256 devices in a mesh: row: 32 (over y_hi, z, core), col: 8 (over x, y_lo).
Axes of the slice: x: 4, y: 4 (y_hi: 2, y_lo: 2; y = y_hi * 2 + y_lo), z: 8, core: 2. Of those that a mesh axis runs over, the one named last changes fastest.
Arguments:
- tokens: bfloat16 [1024, 16384], P('row', 'col'), may hold values from -6 to 6
- cotangent: bfloat16 [1024, 16384], P('row', 'col'), may hold values from -6 to 6
- w_gate: bfloat16 [16384, 12288], P('col', 'row'), may hold values from -0.046875 to 0.046875
- w_up: bfloat16 [16384, 12288], P('col', 'row'), may hold values from -0.046875 to 0.046875
- w_down: bfloat16 [12288, 16384], P('row', 'col'), may hold values from -0.0546875 to 0.0546875
Outputs:
- grad_tokens: bfloat16 [1024, 16384], P('row', 'col')
- grad_w_gate: bfloat16 [16384, 12288], P('col', 'row')
- grad_w_up: bfloat16 [16384, 12288], P('col', 'row')
- grad_w_down: bfloat16 [12288, 16384], P('row', 'col')
The draws below stay inside these ranges and needn't reach their ends.
All inputs are finite; a program needn't handle non-finite values.
Results may differ from the reference program's by a relative error of at most 0.005.
Values may be sent and summed in bfloat16 or wider, within the bound.
A program may use at most 128 MiB of HBM per device.

```python
import jax
import jax.numpy as jnp

D = 16384
FF = 12288
TOKENS = 1024


def level_of(own_key, shape, cuts, low, high):
    def one(position, blocks):
        draws = jax.random.uniform(jax.random.fold_in(jax.random.fold_in(own_key, 6), position), (blocks,), jnp.float32, low / len(cuts), high / len(cuts))
        return jnp.repeat(jnp.exp(draws), shape[position] // blocks).reshape((-1,) + (1,) * (len(shape) - position - 1))

    loudness = one(*cuts[0])
    for cut in cuts[1:]:
        loudness = loudness * one(*cut)
    return loudness


def noise(stream_key, shape, spread, reach, pieces=(), held_as=jnp.bfloat16):
    entries = spread * jax.random.normal(stream_key, shape, jnp.float32)
    if pieces:
        entries = entries * level_of(stream_key, shape, pieces, -0.22, 0.18)
    return jnp.clip(entries, -reach, reach).astype(held_as)


def setup_inputs(seed: int = 0) -> dict:
    arg_keys = jax.random.split(jax.random.key(seed), 6)
    tokens = noise(arg_keys[0], (TOKENS, D), 1.0, 6.0, ((0, 32), (1, 8)))
    cotangent = noise(arg_keys[1], (TOKENS, D), 1.0, 6.0, ((0, 32), (1, 8)))
    w_gate = noise(arg_keys[2], (D, FF), D ** -0.5, 0.046875, ((0, 8), (1, 32)))
    w_up = noise(arg_keys[3], (D, FF), D ** -0.5, 0.046875, ((0, 8), (1, 32)))
    w_down = noise(arg_keys[4], (FF, D), FF ** -0.5, 0.0546875, ((0, 32), (1, 8)))
    return dict(tokens=tokens, cotangent=cotangent, w_gate=w_gate, w_up=w_up, w_down=w_down)


def reference(tokens, cotangent, w_gate, w_up, w_down):
    gate_value = jnp.dot(tokens, w_gate, preferred_element_type=jnp.float32)
    up_value = jnp.dot(tokens, w_up, preferred_element_type=jnp.float32)
    grad_act = jnp.dot(cotangent, w_down.T, preferred_element_type=jnp.float32)
    sigmoid_gate = jax.nn.sigmoid(gate_value)
    silu_gate = gate_value * sigmoid_gate
    activation = (silu_gate * up_value).astype(jnp.bfloat16)
    grad_gate = (grad_act * up_value * sigmoid_gate * (1.0 + gate_value * (1.0 - sigmoid_gate))).astype(jnp.bfloat16)
    grad_up = (grad_act * silu_gate).astype(jnp.bfloat16)
    grad_w_gate = jnp.dot(tokens.T, grad_gate, preferred_element_type=jnp.float32).astype(jnp.bfloat16)
    grad_w_up = jnp.dot(tokens.T, grad_up, preferred_element_type=jnp.float32).astype(jnp.bfloat16)
    grad_w_down = jnp.dot(activation.T, cotangent, preferred_element_type=jnp.float32).astype(jnp.bfloat16)
    grad_tokens = (jnp.dot(grad_gate, w_gate.T, preferred_element_type=jnp.float32) + jnp.dot(grad_up, w_up.T, preferred_element_type=jnp.float32)).astype(jnp.bfloat16)
    return grad_tokens, grad_w_gate, grad_w_up, grad_w_down
```

```python
import jax
import jax.numpy as jnp
from jax import lax
from jax.experimental import pallas as pl
from jax.experimental.pallas import tpu as pltpu
from jax.sharding import PartitionSpec as P

MESH = pl.DeviceIdType.MESH
F32 = jnp.float32
BF16 = jnp.bfloat16

ZN = 8
CN = 8
STEPS = 8
SUB = 64
BLK = 2 * SUB
PIECE = BLK // CN
FEAT = 2048
HID = 384
H3 = 3 * HID
TOK = 32


def dot_nn(a, b):
    return lax.dot_general(a, b, (((1,), (0,)), ((), ())), preferred_element_type=F32)


def dot_nt(a, b):
    return lax.dot_general(a, b, (((1,), (1,)), ((), ())), preferred_element_type=F32)


def dot_tn(a, b):
    return lax.dot_general(a, b, (((0,), (0,)), ((), ())), preferred_element_type=F32)


def kernel(
    x_ref, dy_ref, wg_ref, wu_ref, wd_ref,
    gt_ref, gwg_ref, gwu_ref, gwd_ref,
    t_own, xy, wgu, wd, pf, own, pb, rb, hid, gf, r1, s2, r2, s3, rd, acc, ogu, od,
    w_sem, t_sem, o_sem, ex_s, ex_r, ring_s, ring_r, sib_s, sib_r,
    b_s, b_r, c_s, c_r, d1_s, d1_r, d2_s, d2_r, d3_s, d3_r,
):
    row = lax.axis_index("row")
    col = lax.axis_index("col")
    yh, z, c = row // (2 * ZN), (row // 2) % ZN, row % 2

    def at(dz=0, dyh=0, dc=0):
        return (((yh + dyh) % 2) * (2 * ZN) + ((z + dz + ZN) % ZN) * 2 + (c + dc) % 2, col)

    def colpeer(r):
        return (row, (col + r) % CN)

    sib, partner, cross = at(dc=1), at(dyh=1), at(dyh=1, dc=1)

    loads = [
        pltpu.make_async_copy(wg_ref, wgu.at[:, pl.ds(0, HID)], w_sem.at[0]),
        pltpu.make_async_copy(wu_ref, wgu.at[:, pl.ds(HID, HID)], w_sem.at[1]),
        pltpu.make_async_copy(wd_ref, wd, w_sem.at[2]),
    ]
    for cp in loads:
        cp.start()

    barrier = pltpu.get_barrier_semaphore()
    greet = [sib, partner, cross]
    greet += [at(dz=k) for k in range(1, ZN)]
    greet += [colpeer(r) for r in range(1, CN)]
    for d in greet:
        pl.semaphore_signal(barrier, inc=1, device_id=d, device_id_type=MESH)
    t_own[0] = x_ref[...]
    t_own[1] = dy_ref[...]
    pl.semaphore_wait(barrier, len(greet))

    def remote(src, dst, ss, rs, dev):
        return pltpu.make_async_remote_copy(
            src_ref=src, dst_ref=dst, send_sem=ss, recv_sem=rs, device_id=dev, device_id_type=MESH
        )

    pending = []

    def go(cp):
        cp.start()
        pending.append(cp)
        return cp

    mine = pl.ds(pl.multiple_of(c * TOK, TOK), TOK)
    go(remote(t_own.at[1 - c], xy.at[1 - c, 0, 0, mine], ex_s.at[0], ex_r.at[0], sib))
    go(remote(t_own.at[c], xy.at[c, 0, 1, mine], ex_s.at[1], ex_r.at[1], partner))
    go(remote(t_own.at[1 - c], xy.at[1 - c, 0, 1, mine], ex_s.at[2], ex_r.at[2], cross))
    keep = pltpu.make_async_copy(t_own.at[c], xy.at[c, 0, 0, mine], t_sem)
    keep.start()

    theirs = pl.ds(pl.multiple_of((1 - c) * TOK, TOK), TOK)

    def arrived(src, dst, ss, rs):
        remote(src, dst, ss, rs, sib).wait_recv()

    nxt = (at(dz=1), at(dz=-1))

    def send_ring(src_step, src_half, dst_step, d):
        go(
            remote(
                xy.at[c, src_step, src_half], xy.at[c, dst_step, d],
                ring_s.at[dst_step - 1, d], ring_r.at[dst_step - 1, d], nxt[d],
            )
        )

    def stage_gather(s):
        if s == 0:
            keep.wait()
            arrived(t_own.at[0], xy.at[c, 0, 0, theirs], ex_s.at[0], ex_r.at[0])
            send_ring(0, 0, 1, 0)
            send_ring(0, 0, 1, 1)
            arrived(t_own.at[0], xy.at[c, 0, 1, mine], ex_s.at[1], ex_r.at[1])
            arrived(t_own.at[0], xy.at[c, 0, 1, theirs], ex_s.at[2], ex_r.at[2])
            send_ring(0, 1, 2, 0)
            send_ring(0, 1, 2, 1)
        else:
            for d in range(2):
                arrived(xy.at[c, s, d], xy.at[c, s, d], ring_s.at[s - 1, d], ring_r.at[s - 1, d])
                if s <= 4 or (s == 5 and d == 0) or (s == 6 and d == 1):
                    send_ring(s, d, 7 if s >= 5 else s + 2, d)
        go(remote(xy.at[c, s], xy.at[c, s], sib_s.at[s], sib_r.at[s], sib))

    me16 = pl.ds(pl.multiple_of(col * PIECE, PIECE), PIECE)

    def stage_forward(s):
        arrived(xy.at[1 - c, s], xy.at[1 - c, s], sib_s.at[s], sib_r.at[s])
        if s == 0:
            for cp in loads:
                cp.wait()
        pf[:, : 2 * HID] = dot_nn(xy[0, s].reshape(BLK, FEAT), wgu[...])
        pf[:, 2 * HID :] = dot_nt(xy[1, s].reshape(BLK, FEAT), wd[...])
        pb[s] = pf[...].astype(BF16)
        own[s] = pf[me16, :]
        for r in range(1, CN):
            q = (col + r) % CN
            go(
                remote(
                    pb.at[s, pl.ds(pl.multiple_of(q * PIECE, PIECE), PIECE)], rb.at[s, r - 1],
                    b_s.at[s, r - 1], b_r.at[s, r - 1], colpeer(r),
                )
            )

    def stage_hidden(s):
        total = own[s]
        for r in range(1, CN):
            arrived(rb.at[s, r - 1], rb.at[s, r - 1], b_s.at[s, r - 1], b_r.at[s, r - 1])
            total = total + rb[s, r - 1].astype(F32)
        gate_value = total[:, :HID]
        up_value = total[:, HID : 2 * HID]
        grad_act = total[:, 2 * HID :]
        sig = jax.nn.sigmoid(gate_value)
        silu = gate_value * sig
        hid[s, me16, pl.ds(0, HID)] = (
            grad_act * up_value * sig * (1.0 + gate_value * (1.0 - sig))
        ).astype(BF16)
        hid[s, me16, pl.ds(HID, HID)] = (grad_act * silu).astype(BF16)
        hid[s, me16, pl.ds(2 * HID, HID)] = (silu * up_value).astype(BF16)
        for r in range(1, CN):
            go(remote(hid.at[s, me16], hid.at[s, me16], c_s.at[s, r - 1], c_r.at[s, r - 1], colpeer(r)))

    def stage_tokens(s):
        for r in range(1, CN):
            q = (col - r + CN) % CN
            piece = hid.at[s, pl.ds(pl.multiple_of(q * PIECE, PIECE), PIECE)]
            arrived(piece, piece, c_s.at[s, r - 1], c_r.at[s, r - 1])
        gf[s] = dot_nt(hid[s, :, : 2 * HID], wgu[...]).reshape(2, 2, TOK, FEAT)
        for d in range(2):
            go(remote(gf.at[s, d, 1 - c], r1.at[s, d], d1_s.at[s, d], d1_r.at[s, d], sib))

    def stage_pair(s):
        for d in range(2):
            arrived(r1.at[s, d], r1.at[s, d], d1_s.at[s, d], d1_r.at[s, d])
        for d in range(2):
            v = gf[s, d, c] + r1[s, d]
            other = d == 1 if s in (0, 7) else s % 2 == 0
            if other:
                k = (s + 1) // 2
                s2[k, d] = v.astype(BF16)
                go(remote(s2.at[k, d], r2.at[k, d], d2_s.at[k, d], d2_r.at[k, d], partner))
            else:
                acc[(s + 1) // 2, d] = v

    def stage_home(k):
        for d in range(2):
            src = 1 if k in (0, 4) else d
            if k in (0, 4) and d == 1:
                continue
            arrived(r2.at[k, src], r2.at[k, src], d2_s.at[k, src], d2_r.at[k, src])
            v = acc[k, d] + r2[k, src].astype(F32)
            if k == 0:
                acc[0, 0] = v
            else:
                slot = 2 * (k - 1) + d
                s3[slot] = v.astype(BF16)
                dest = at(dz=k if d else -k)
                go(remote(s3.at[slot], rd.at[slot], d3_s.at[slot], d3_r.at[slot], dest))

    outs = []

    def weight_grads(which):
        hs = hid[...].reshape(STEPS * BLK, H3)
        if which < 2:
            for m in range(4):
                f = (which * 4 + m) * 256
                ogu[pl.ds(f, 256), :] = dot_tn(
                    xy[0, :, :, :, f : f + 256].reshape(STEPS * BLK, 256), hs[:, : 2 * HID]
                ).astype(BF16)
        else:
            for m in range(8):
                f = m * 256
                od[:, pl.ds(f, 256)] = dot_tn(
                    hs[:, 2 * HID :], xy[1, :, :, :, f : f + 256].reshape(STEPS * BLK, 256)
                ).astype(BF16)
        if which == 1:
            outs.append(pltpu.make_async_copy(ogu.at[:, pl.ds(0, HID)], gwg_ref, o_sem.at[0]))
            outs.append(pltpu.make_async_copy(ogu.at[:, pl.ds(HID, HID)], gwu_ref, o_sem.at[1]))
            outs[0].start()
            outs[1].start()
        if which == 2:
            outs.append(pltpu.make_async_copy(od, gwd_ref, o_sem.at[2]))
            outs[2].start()

    for i in range(STEPS + 4):
        if i < STEPS:
            stage_gather(i)
        if 0 <= i - 3 < STEPS:
            stage_pair(i - 3)
        if i < STEPS:
            stage_forward(i)
        if 0 <= i - 1 < STEPS:
            stage_hidden(i - 1)
        if 0 <= i - 2 < STEPS:
            stage_tokens(i - 2)
        j = i - 4
        if 0 <= j < STEPS and (j % 2 == 0 or j == 7):
            stage_home((j + 1) // 2)
        if i >= STEPS + 1:
            weight_grads(i - STEPS - 1)

    total = acc[0, 0]
    for slot in range(ZN - 1):
        arrived(rd.at[slot], rd.at[slot], d3_s.at[slot], d3_r.at[slot])
        total = total + rd[slot].astype(F32)
    gt_ref[...] = total.astype(BF16)
    for cp in pending:
        cp.wait_send()
    for cp in outs:
        cp.wait()


def local(tokens, cotangent, w_gate, w_up, w_down):
    dma = pltpu.SemaphoreType.DMA
    vm = pltpu.VMEM
    any_spec = pl.BlockSpec(memory_space=pl.ANY)
    vmem_spec = pl.BlockSpec(memory_space=pltpu.VMEM)
    return pl.pallas_call(
        kernel,
        out_shape=(
            jax.ShapeDtypeStruct((TOK, FEAT), BF16),
            jax.ShapeDtypeStruct((FEAT, HID), BF16),
            jax.ShapeDtypeStruct((FEAT, HID), BF16),
            jax.ShapeDtypeStruct((HID, FEAT), BF16),
        ),
        in_specs=[vmem_spec, vmem_spec, any_spec, any_spec, any_spec],
        out_specs=(vmem_spec, any_spec, any_spec, any_spec),
        scratch_shapes=[
            vm((2, TOK, FEAT), BF16),
            vm((2, STEPS, 2, SUB, FEAT), BF16),
            vm((FEAT, 2 * HID), BF16),
            vm((HID, FEAT), BF16),
            vm((BLK, H3), F32),
            vm((STEPS, PIECE, H3), F32),
            vm((STEPS, BLK, H3), BF16),
            vm((STEPS, CN - 1, PIECE, H3), BF16),
            vm((STEPS, BLK, H3), BF16),
            vm((STEPS, 2, 2, TOK, FEAT), F32),
            vm((STEPS, 2, TOK, FEAT), F32),
            vm((5, 2, TOK, FEAT), BF16),
            vm((5, 2, TOK, FEAT), BF16),
            vm((ZN - 1, TOK, FEAT), BF16),
            vm((ZN - 1, TOK, FEAT), BF16),
            vm((5, 2, TOK, FEAT), F32),
            vm((FEAT, 2 * HID), BF16),
            vm((HID, FEAT), BF16),
            dma((3,)),
            dma(()),
            dma((3,)),
            dma((3,)),
            dma((3,)),
            dma((7, 2)),
            dma((7, 2)),
            dma((STEPS,)),
            dma((STEPS,)),
            dma((STEPS, CN - 1)),
            dma((STEPS, CN - 1)),
            dma((STEPS, CN - 1)),
            dma((STEPS, CN - 1)),
            dma((STEPS, 2)),
            dma((STEPS, 2)),
            dma((5, 2)),
            dma((5, 2)),
            dma((7,)),
            dma((7,)),
        ],
        compiler_params=pltpu.CompilerParams(
            collective_id=0, has_side_effects=True, vmem_limit_bytes=60 * 2**20
        ),
        cost_estimate=pl.CostEstimate(
            flops=13 * 10**9, bytes_accessed=10**7, transcendentals=5 * 10**4
        ),
        name="swiglu_backward",
    )(tokens, cotangent, w_gate, w_up, w_down)


def solution(mesh):
    placed = (P("row", "col"), P("row", "col"), P("col", "row"), P("col", "row"), P("row", "col"))
    return jax.shard_map(
        local,
        mesh=mesh,
        in_specs=placed,
        out_specs=(P("row", "col"), P("col", "row"), P("col", "row"), P("row", "col")),
        check_vma=False,
    )
```

```python
import jax
import jax.numpy as jnp
from jax import lax
from jax.experimental import pallas as pl
from jax.experimental.pallas import tpu as pltpu
from jax.sharding import PartitionSpec as P

MESH = pl.DeviceIdType.MESH
F32 = jnp.float32
BF16 = jnp.bfloat16

ZN = 8
CN = 8
STEPS = 8
SUB = 64
BLK = 2 * SUB
PIECE = BLK // CN
FEAT = 2048
HID = 384
H3 = 3 * HID
TOK = 32
HALF = FEAT // 2


def dot_nn(a, b):
    return lax.dot_general(a, b, (((1,), (0,)), ((), ())), preferred_element_type=F32)


def dot_nt(a, b):
    return lax.dot_general(a, b, (((1,), (1,)), ((), ())), preferred_element_type=F32)


def dot_tn(a, b):
    return lax.dot_general(a, b, (((0,), (0,)), ((), ())), preferred_element_type=F32)


def kernel(
    x_ref, dy_ref, wg_ref, wu_ref, wd_ref,
    gt_ref, gwg_ref, gwu_ref, gwd_ref,
    t_own, xy, wgu, wd, pf, own, pb, rb, hid, gf, r1, s2, r2, s3, rd, s4, r4, acc,
    w_sem, t_sem, ex_s, ex_r, ring_s, ring_r, sib_s, sib_r,
    b_s, b_r, c_s, c_r, d1_s, d1_r, d2_s, d2_r, d3_s, d3_r, d4_s, d4_r,
):
    row = lax.axis_index("row")
    col = lax.axis_index("col")
    yh, z, c = row // (2 * ZN), (row // 2) % ZN, row % 2

    def at(dz=0, dyh=0, dc=0):
        return (((yh + dyh) % 2) * (2 * ZN) + ((z + dz + ZN) % ZN) * 2 + (c + dc) % 2, col)

    def colpeer(r):
        return (row, (col + r) % CN)

    def colat(dx=0, dyl=0):
        return ((col // 2 + dx) % (CN // 2)) * 2 + (col % 2 + dyl) % 2

    def rows16(q):
        return pl.ds(pl.multiple_of(q * PIECE, PIECE), PIECE)

    sib, partner, cross = at(dc=1), at(dyh=1), at(dyh=1, dc=1)

    loads = [
        pltpu.make_async_copy(wg_ref, wgu.at[:, pl.ds(0, HID)], w_sem.at[0]),
        pltpu.make_async_copy(wu_ref, wgu.at[:, pl.ds(HID, HID)], w_sem.at[1]),
        pltpu.make_async_copy(wd_ref, wd, w_sem.at[2]),
    ]
    for cp in loads:
        cp.start()

    barrier = pltpu.get_barrier_semaphore()
    greet = [sib, partner, cross]
    greet += [at(dz=k) for k in (1, 2, -2, -1)]
    greet += [colpeer(r) for r in range(1, CN)]
    for d in greet:
        pl.semaphore_signal(barrier, inc=1, device_id=d, device_id_type=MESH)
    t_own[0] = x_ref[...]
    t_own[1] = dy_ref[...]
    pl.semaphore_wait(barrier, len(greet))

    def remote(src, dst, ss, rs, dev):
        return pltpu.make_async_remote_copy(
            src_ref=src, dst_ref=dst, send_sem=ss, recv_sem=rs, device_id=dev, device_id_type=MESH
        )

    pending = []

    def go(cp):
        cp.start()
        pending.append(cp)
        return cp

    mine = pl.ds(pl.multiple_of(c * TOK, TOK), TOK)
    go(remote(t_own.at[1 - c], xy.at[1 - c, 0, 0, mine], ex_s.at[0], ex_r.at[0], sib))
    go(remote(t_own.at[c], xy.at[c, 0, 1, mine], ex_s.at[1], ex_r.at[1], partner))
    go(remote(t_own.at[1 - c], xy.at[1 - c, 0, 1, mine], ex_s.at[2], ex_r.at[2], cross))
    keep = pltpu.make_async_copy(t_own.at[c], xy.at[c, 0, 0, mine], t_sem)
    keep.start()

    theirs = pl.ds(pl.multiple_of((1 - c) * TOK, TOK), TOK)

    def arrived(src, dst, ss, rs):
        remote(src, dst, ss, rs, sib).wait_recv()

    nxt = (at(dz=1), at(dz=-1))

    def send_ring(src_step, src_half, dst_step, d):
        go(
            remote(
                xy.at[c, src_step, src_half], xy.at[c, dst_step, d],
                ring_s.at[dst_step - 1, d], ring_r.at[dst_step - 1, d], nxt[d],
            )
        )

    def stage_gather(s):
        if s == 0:
            keep.wait()
            arrived(t_own.at[0], xy.at[c, 0, 0, theirs], ex_s.at[0], ex_r.at[0])
            send_ring(0, 0, 1, 0)
            send_ring(0, 0, 1, 1)
            arrived(t_own.at[0], xy.at[c, 0, 1, mine], ex_s.at[1], ex_r.at[1])
            arrived(t_own.at[0], xy.at[c, 0, 1, theirs], ex_s.at[2], ex_r.at[2])
            send_ring(0, 1, 2, 0)
            send_ring(0, 1, 2, 1)
        else:
            for d in range(2):
                arrived(xy.at[c, s, d], xy.at[c, s, d], ring_s.at[s - 1, d], ring_r.at[s - 1, d])
                if s <= 4 or (s == 5 and d == 0) or (s == 6 and d == 1):
                    send_ring(s, d, 7 if s >= 5 else s + 2, d)
        go(remote(xy.at[c, s], xy.at[c, s], sib_s.at[s], sib_r.at[s], sib))

    me16 = pl.ds(pl.multiple_of(col * PIECE, PIECE), PIECE)

    def stage_forward(s):
        arrived(xy.at[1 - c, s], xy.at[1 - c, s], sib_s.at[s], sib_r.at[s])
        if s == 0:
            for cp in loads:
                cp.wait()
        pf[:, : 2 * HID] = dot_nn(xy[0, s].reshape(BLK, FEAT), wgu[...])
        pf[:, 2 * HID :] = dot_nt(xy[1, s].reshape(BLK, FEAT), wd[...])
        pb[s] = pf[...].astype(BF16)
        own[s] = pf[me16, :]
        for r in range(1, CN):
            q = (col + r) % CN
            go(
                remote(
                    pb.at[s, pl.ds(pl.multiple_of(q * PIECE, PIECE), PIECE)], rb.at[s, r - 1],
                    b_s.at[s, r - 1], b_r.at[s, r - 1], colpeer(r),
                )
            )

    def stage_hidden(s):
        total = own[s]
        for r in range(1, CN):
            arrived(rb.at[s, r - 1], rb.at[s, r - 1], b_s.at[s, r - 1], b_r.at[s, r - 1])
            total = total + rb[s, r - 1].astype(F32)
        gate_value = total[:, :HID]
        up_value = total[:, HID : 2 * HID]
        grad_act = total[:, 2 * HID :]
        sig = jax.nn.sigmoid(gate_value)
        silu = gate_value * sig
        hid[s, me16, pl.ds(0, HID)] = (
            grad_act * up_value * sig * (1.0 + gate_value * (1.0 - sig))
        ).astype(BF16)
        hid[s, me16, pl.ds(HID, HID)] = (grad_act * silu).astype(BF16)
        hid[s, me16, pl.ds(2 * HID, HID)] = (silu * up_value).astype(BF16)
        go(remote(hid.at[s, me16], hid.at[s, me16], c_s.at[s, 0], c_r.at[s, 0], (row, colat(dyl=1))))
        send_x(s, me16, 0)

    def send_x(s, rows, base):
        for dx in range(1, CN // 2):
            q = base + dx
            go(remote(hid.at[s, rows], hid.at[s, rows], c_s.at[s, q], c_r.at[s, q], (row, colat(dx=dx))))

    def stage_relay(s):
        piece = rows16(colat(dyl=1))
        arrived(hid.at[s, piece], hid.at[s, piece], c_s.at[s, 0], c_r.at[s, 0])
        send_x(s, piece, 3)

    def stage_tokens(s):
        for dx in range(1, CN // 2):
            for dyl in range(2):
                piece = hid.at[s, rows16(colat(dx=CN // 2 - dx, dyl=dyl))]
                q = 3 * dyl + dx
                arrived(piece, piece, c_s.at[s, q], c_r.at[s, q])
        gf[s] = dot_nt(hid[s, :, : 2 * HID], wgu[...]).reshape(2, 2, TOK, FEAT)
        for d in range(2):
            go(remote(gf.at[s, d, 1 - c], r1.at[s, d], d1_s.at[s, d], d1_r.at[s, d], sib))

    def stage_pair(s):
        for d in range(2):
            arrived(r1.at[s, d], r1.at[s, d], d1_s.at[s, d], d1_r.at[s, d])
        for d in range(2):
            v = gf[s, d, c] + r1[s, d]
            other = d == 1 if s in (0, 7) else s % 2 == 0
            if other:
                k = (s + 1) // 2
                s2[k, d] = v.astype(BF16)
                go(remote(s2.at[k, d], r2.at[k, d], d2_s.at[k, d], d2_r.at[k, d], partner))
            else:
                acc[(s + 1) // 2, d] = v

    def hop(slot, dz):
        go(remote(s3.at[slot], rd.at[slot], d3_s.at[slot], d3_r.at[slot], at(dz=dz)))

    def landed(slot):
        arrived(rd.at[slot], rd.at[slot], d3_s.at[slot], d3_r.at[slot])
        return rd[slot].astype(F32)

    def stage_home(k):
        if k in (0, 4):
            arrived(r2.at[k, 1], r2.at[k, 1], d2_s.at[k, 1], d2_r.at[k, 1])
            v = acc[k, 0] + r2[k, 1].astype(F32)
            if k == 0:
                acc[0, 0] = v
                return
            for d in range(2):
                s4[d] = v[:, d * HALF : (d + 1) * HALF].astype(BF16)
                go(remote(s4.at[d], r4.at[d], d4_s.at[d], d4_r.at[d], at(dz=2 if d else -2)))
            return
        for d in range(2):
            arrived(r2.at[k, d], r2.at[k, d], d2_s.at[k, d], d2_r.at[k, d])
            v = acc[k, d] + r2[k, d].astype(F32)
            if k == 2:
                acc[2, d] = v
            else:
                slot = k - 1 + d
                s3[slot] = v.astype(BF16)
                hop(slot, 1 if d else -1)

    def stage_join():
        for d in range(2):
            acc[2, d] = acc[2, d] + landed(2 + d)
        for d in range(2):
            part = pl.ds(d * HALF, HALF)
            arrived(r4.at[d], r4.at[d], d4_s.at[d], d4_r.at[d])
            acc[2, d, :, part] = acc[2, d, :, part] + r4[d].astype(F32)
            s3[4 + d] = acc[2, d].astype(BF16)
            hop(4 + d, 2 if d else -2)

    def weight_grads(which):
        hs = hid[...].reshape(STEPS * BLK, H3)
        if which < 2:
            for m in range(4):
                f = (which * 4 + m) * 256
                g = dot_tn(
                    xy[0, :, :, :, f : f + 256].reshape(STEPS * BLK, 256), hs[:, : 2 * HID]
                ).astype(BF16)
                gwg_ref[pl.ds(f, 256), :] = g[:, :HID]
                gwu_ref[pl.ds(f, 256), :] = g[:, HID:]
        else:
            for m in range(8):
                f = m * 256
                gwd_ref[:, pl.ds(f, 256)] = dot_tn(
                    hs[:, 2 * HID :], xy[1, :, :, :, f : f + 256].reshape(STEPS * BLK, 256)
                ).astype(BF16)

    for i in range(STEPS + 5):
        if i < STEPS:
            stage_gather(i)
        if 0 <= i - 4 < STEPS:
            stage_pair(i - 4)
        if i < STEPS:
            stage_forward(i)
        if 0 <= i - 1 < STEPS:
            stage_hidden(i - 1)
        if 0 <= i - 2 < STEPS:
            stage_relay(i - 2)
        if 0 <= i - 3 < STEPS:
            stage_tokens(i - 3)
        j = i - 5
        if 0 <= j < STEPS and (j % 2 == 0 or j == 7):
            stage_home((j + 1) // 2)
        if i == STEPS + 3:
            weight_grads(0)
            weight_grads(1)

    stage_join()
    weight_grads(2)
    total = acc[0, 0] + landed(0) + landed(1)
    gt_ref[...] = (total + landed(4) + landed(5)).astype(BF16)
    for cp in pending:
        cp.wait_send()


def store_kernel(a, b, c, d, oa, ob, oc, od, sems):
    copies = [
        pltpu.make_async_copy(src, dst, sems.at[i])
        for i, (src, dst) in enumerate(((a, oa), (b, ob), (c, oc), (d, od)))
    ]
    for cp in copies:
        cp.start()
    for cp in copies:
        cp.wait()


def store(arrays):
    anywhere = pl.BlockSpec(memory_space=pl.ANY)
    return pl.pallas_call(
        store_kernel,
        out_shape=tuple(jax.ShapeDtypeStruct(a.shape, a.dtype) for a in arrays),
        in_specs=[anywhere] * 4,
        out_specs=(anywhere,) * 4,
        scratch_shapes=[pltpu.SemaphoreType.DMA((4,))],
        compiler_params=pltpu.CompilerParams(vmem_limit_bytes=2**20),
        name="store_results",
    )(*arrays)


def local(tokens, cotangent, w_gate, w_up, w_down):
    dma = pltpu.SemaphoreType.DMA
    vm = pltpu.VMEM
    any_spec = pl.BlockSpec(memory_space=pl.ANY)
    vmem_spec = pl.BlockSpec(memory_space=pltpu.VMEM)
    results = pl.pallas_call(
        kernel,
        out_shape=(
            jax.ShapeDtypeStruct((TOK, FEAT), BF16),
            jax.ShapeDtypeStruct((FEAT, HID), BF16),
            jax.ShapeDtypeStruct((FEAT, HID), BF16),
            jax.ShapeDtypeStruct((HID, FEAT), BF16),
        ),
        in_specs=[vmem_spec, vmem_spec, any_spec, any_spec, any_spec],
        out_specs=(vmem_spec,) * 4,
        scratch_shapes=[
            vm((2, TOK, FEAT), BF16),
            vm((2, STEPS, 2, SUB, FEAT), BF16),
            vm((FEAT, 2 * HID), BF16),
            vm((HID, FEAT), BF16),
            vm((BLK, H3), F32),
            vm((STEPS, PIECE, H3), F32),
            vm((STEPS, BLK, H3), BF16),
            vm((STEPS, CN - 1, PIECE, H3), BF16),
            vm((STEPS, BLK, H3), BF16),
            vm((STEPS, 2, 2, TOK, FEAT), F32),
            vm((STEPS, 2, TOK, FEAT), F32),
            vm((5, 2, TOK, FEAT), BF16),
            vm((5, 2, TOK, FEAT), BF16),
            vm((6, TOK, FEAT), BF16),
            vm((6, TOK, FEAT), BF16),
            vm((2, TOK, HALF), BF16),
            vm((2, TOK, HALF), BF16),
            vm((5, 2, TOK, FEAT), F32),
            dma((3,)),
            dma(()),
            dma((3,)),
            dma((3,)),
            dma((7, 2)),
            dma((7, 2)),
            dma((STEPS,)),
            dma((STEPS,)),
            dma((STEPS, CN - 1)),
            dma((STEPS, CN - 1)),
            dma((STEPS, CN - 1)),
            dma((STEPS, CN - 1)),
            dma((STEPS, 2)),
            dma((STEPS, 2)),
            dma((5, 2)),
            dma((5, 2)),
            dma((6,)),
            dma((6,)),
            dma((2,)),
            dma((2,)),
        ],
        compiler_params=pltpu.CompilerParams(
            collective_id=0, has_side_effects=True, vmem_limit_bytes=48 * 2**20
        ),
        cost_estimate=pl.CostEstimate(
            flops=13 * 10**9, bytes_accessed=10**7, transcendentals=5 * 10**4
        ),
        name="swiglu_backward",
    )(tokens, cotangent, w_gate, w_up, w_down)
    return store(results)


def solution(mesh):
    placed = (P("row", "col"), P("row", "col"), P("col", "row"), P("col", "row"), P("row", "col"))
    return jax.shard_map(
        local,
        mesh=mesh,
        in_specs=placed,
        out_specs=(P("row", "col"), P("col", "row"), P("col", "row"), P("row", "col")),
        check_vma=False,
    )
```

```python
import jax
import jax.numpy as jnp
from jax import lax
from jax.experimental import pallas as pl
from jax.experimental.pallas import tpu as pltpu
from jax.sharding import PartitionSpec as P

MESH = pl.DeviceIdType.MESH
F32 = jnp.float32
BF16 = jnp.bfloat16

ZN = 8
CN = 8
STEPS = 8
SUB = 64
BLK = 2 * SUB
PIECE = BLK // CN
FEAT = 2048
HID = 384
H3 = 3 * HID
TOK = 32
HALF = FEAT // 2


def dot_nn(a, b):
    return lax.dot_general(a, b, (((1,), (0,)), ((), ())), preferred_element_type=F32)


def dot_nt(a, b):
    return lax.dot_general(a, b, (((1,), (1,)), ((), ())), preferred_element_type=F32)


def dot_tn(a, b):
    return lax.dot_general(a, b, (((0,), (0,)), ((), ())), preferred_element_type=F32)


def kernel(
    x_ref, dy_ref, wg_ref, wu_ref, wd_ref,
    gt_ref, gwg_ref, gwu_ref, gwd_ref,
    t_own, xy, wgu, wd, pf, own, pb, rb, hid, gf, r1, s2, r2, s3, rd, s4, r4, acc,
    w_sem, t_sem, ex_s, ex_r, ring_s, ring_r, sib_s, sib_r,
    b_s, b_r, c_s, c_r, d1_s, d1_r, d2_s, d2_r, d3_s, d3_r, d4_s, d4_r,
):
    row = lax.axis_index("row")
    col = lax.axis_index("col")
    yh, z, c = row // (2 * ZN), (row // 2) % ZN, row % 2

    def at(dz=0, dyh=0, dc=0):
        return (((yh + dyh) % 2) * (2 * ZN) + ((z + dz + ZN) % ZN) * 2 + (c + dc) % 2, col)

    def colpeer(r):
        return (row, (col + r) % CN)

    def colat(dx=0, dyl=0):
        return ((col // 2 + dx) % (CN // 2)) * 2 + (col % 2 + dyl) % 2

    def rows16(q):
        return pl.ds(pl.multiple_of(q * PIECE, PIECE), PIECE)

    sib, partner, cross = at(dc=1), at(dyh=1), at(dyh=1, dc=1)

    loads = [
        pltpu.make_async_copy(wg_ref, wgu.at[:, pl.ds(0, HID)], w_sem.at[0]),
        pltpu.make_async_copy(wu_ref, wgu.at[:, pl.ds(HID, HID)], w_sem.at[1]),
        pltpu.make_async_copy(wd_ref, wd, w_sem.at[2]),
    ]
    for cp in loads:
        cp.start()

    barrier = pltpu.get_barrier_semaphore()
    greet = [sib, partner, cross]
    greet += [at(dz=k) for k in (1, 2, -2, -1)]
    greet += [colpeer(r) for r in range(1, CN)]
    for d in greet:
        pl.semaphore_signal(barrier, inc=1, device_id=d, device_id_type=MESH)
    t_own[0] = x_ref[...]
    t_own[1] = dy_ref[...]
    pl.semaphore_wait(barrier, len(greet))

    def remote(src, dst, ss, rs, dev):
        return pltpu.make_async_remote_copy(
            src_ref=src, dst_ref=dst, send_sem=ss, recv_sem=rs, device_id=dev, device_id_type=MESH
        )

    pending = []

    def go(cp):
        cp.start()
        pending.append(cp)
        return cp

    mine = pl.ds(pl.multiple_of(c * TOK, TOK), TOK)
    go(remote(t_own.at[1 - c], xy.at[1 - c, 0, 0, mine], ex_s.at[0], ex_r.at[0], sib))
    go(remote(t_own.at[c], xy.at[c, 0, 1, mine], ex_s.at[1], ex_r.at[1], partner))
    go(remote(t_own.at[1 - c], xy.at[1 - c, 0, 1, mine], ex_s.at[2], ex_r.at[2], cross))
    keep = pltpu.make_async_copy(t_own.at[c], xy.at[c, 0, 0, mine], t_sem)
    keep.start()

    theirs = pl.ds(pl.multiple_of((1 - c) * TOK, TOK), TOK)

    def arrived(src, dst, ss, rs):
        remote(src, dst, ss, rs, sib).wait_recv()

    nxt = (at(dz=1), at(dz=-1))

    def send_ring(src_step, src_half, dst_step, d):
        go(
            remote(
                xy.at[c, src_step, src_half], xy.at[c, dst_step, d],
                ring_s.at[dst_step - 1, d], ring_r.at[dst_step - 1, d], nxt[d],
            )
        )

    def stage_gather(s):
        if s == 0:
            keep.wait()
            arrived(t_own.at[0], xy.at[c, 0, 0, theirs], ex_s.at[0], ex_r.at[0])
            send_ring(0, 0, 1, 0)
            send_ring(0, 0, 1, 1)
            arrived(t_own.at[0], xy.at[c, 0, 1, mine], ex_s.at[1], ex_r.at[1])
            arrived(t_own.at[0], xy.at[c, 0, 1, theirs], ex_s.at[2], ex_r.at[2])
            send_ring(0, 1, 2, 0)
            send_ring(0, 1, 2, 1)
        else:
            for d in range(2):
                arrived(xy.at[c, s, d], xy.at[c, s, d], ring_s.at[s - 1, d], ring_r.at[s - 1, d])
                if s <= 4 or (s == 5 and d == 0) or (s == 6 and d == 1):
                    send_ring(s, d, 7 if s >= 5 else s + 2, d)
        go(remote(xy.at[c, s], xy.at[c, s], sib_s.at[s], sib_r.at[s], sib))

    me16 = pl.ds(pl.multiple_of(col * PIECE, PIECE), PIECE)

    def stage_forward(s):
        arrived(xy.at[1 - c, s], xy.at[1 - c, s], sib_s.at[s], sib_r.at[s])
        if s == 0:
            for cp in loads:
                cp.wait()
        pf[:, : 2 * HID] = dot_nn(xy[0, s].reshape(BLK, FEAT), wgu[...])
        pf[:, 2 * HID :] = dot_nt(xy[1, s].reshape(BLK, FEAT), wd[...])
        pb[s] = pf[...].astype(BF16)
        own[s] = pf[me16, :]
        for r in range(1, CN):
            q = (col + r) % CN
            go(
                remote(
                    pb.at[s, pl.ds(pl.multiple_of(q * PIECE, PIECE), PIECE)], rb.at[s, r - 1],
                    b_s.at[s, r - 1], b_r.at[s, r - 1], colpeer(r),
                )
            )

    def stage_hidden(s):
        total = own[s]
        for r in range(1, CN):
            arrived(rb.at[s, r - 1], rb.at[s, r - 1], b_s.at[s, r - 1], b_r.at[s, r - 1])
            total = total + rb[s, r - 1].astype(F32)
        gate_value = total[:, :HID]
        up_value = total[:, HID : 2 * HID]
        grad_act = total[:, 2 * HID :]
        sig = jax.nn.sigmoid(gate_value)
        silu = gate_value * sig
        hid[s, me16, pl.ds(0, HID)] = (
            grad_act * up_value * sig * (1.0 + gate_value * (1.0 - sig))
        ).astype(BF16)
        hid[s, me16, pl.ds(HID, HID)] = (grad_act * silu).astype(BF16)
        hid[s, me16, pl.ds(2 * HID, HID)] = (silu * up_value).astype(BF16)
        go(remote(hid.at[s, me16], hid.at[s, me16], c_s.at[s, 0], c_r.at[s, 0], (row, colat(dyl=1))))
        send_x(s, me16, 0)

    def send_x(s, rows, base):
        for dx in range(1, CN // 2):
            q = base + dx
            go(remote(hid.at[s, rows], hid.at[s, rows], c_s.at[s, q], c_r.at[s, q], (row, colat(dx=dx))))

    def stage_relay(s):
        piece = rows16(colat(dyl=1))
        arrived(hid.at[s, piece], hid.at[s, piece], c_s.at[s, 0], c_r.at[s, 0])
        send_x(s, piece, 3)

    def stage_tokens(s):
        for dx in range(1, CN // 2):
            for dyl in range(2):
                piece = hid.at[s, rows16(colat(dx=CN // 2 - dx, dyl=dyl))]
                q = 3 * dyl + dx
                arrived(piece, piece, c_s.at[s, q], c_r.at[s, q])
        gf[s] = dot_nt(hid[s, :, : 2 * HID], wgu[...]).reshape(2, 2, TOK, FEAT)
        for d in range(2):
            go(remote(gf.at[s, d, 1 - c], r1.at[s, d], d1_s.at[s, d], d1_r.at[s, d], sib))

    def stage_pair(s):
        for d in range(2):
            arrived(r1.at[s, d], r1.at[s, d], d1_s.at[s, d], d1_r.at[s, d])
        for d in range(2):
            v = gf[s, d, c] + r1[s, d]
            other = d == 1 if s in (0, 7) else s % 2 == 0
            if other:
                k = (s + 1) // 2
                s2[k, d] = v.astype(BF16)
                go(remote(s2.at[k, d], r2.at[k, d], d2_s.at[k, d], d2_r.at[k, d], partner))
            else:
                acc[(s + 1) // 2, d] = v

    def hop(slot, dz):
        go(remote(s3.at[slot], rd.at[slot], d3_s.at[slot], d3_r.at[slot], at(dz=dz)))

    def landed(slot):
        arrived(rd.at[slot], rd.at[slot], d3_s.at[slot], d3_r.at[slot])
        return rd[slot].astype(F32)

    def stage_home(k):
        if k in (0, 4):
            arrived(r2.at[k, 1], r2.at[k, 1], d2_s.at[k, 1], d2_r.at[k, 1])
            v = acc[k, 0] + r2[k, 1].astype(F32)
            if k == 0:
                acc[0, 0] = v
                return
            for d in range(2):
                s4[d] = v[:, d * HALF : (d + 1) * HALF].astype(BF16)
                go(remote(s4.at[d], r4.at[d], d4_s.at[d], d4_r.at[d], at(dz=2 if d else -2)))
            return
        for d in range(2):
            arrived(r2.at[k, d], r2.at[k, d], d2_s.at[k, d], d2_r.at[k, d])
            v = acc[k, d] + r2[k, d].astype(F32)
            if k == 2:
                acc[2, d] = v
            else:
                slot = k - 1 + d
                s3[slot] = v.astype(BF16)
                hop(slot, 1 if d else -1)

    def stage_join():
        for d in range(2):
            acc[2, d] = acc[2, d] + landed(2 + d)
        for d in range(2):
            part = pl.ds(d * HALF, HALF)
            arrived(r4.at[d], r4.at[d], d4_s.at[d], d4_r.at[d])
            acc[2, d, :, part] = acc[2, d, :, part] + r4[d].astype(F32)
            s3[4 + d] = acc[2, d].astype(BF16)
            hop(4 + d, 2 if d else -2)

    def weight_grads(which):
        hs = hid[...].reshape(STEPS * BLK, H3)
        if which < 2:
            for m in range(4):
                f = (which * 4 + m) * 256
                g = dot_tn(
                    xy[0, :, :, :, f : f + 256].reshape(STEPS * BLK, 256), hs[:, : 2 * HID]
                ).astype(BF16)
                gwg_ref[pl.ds(f, 256), :] = g[:, :HID]
                gwu_ref[pl.ds(f, 256), :] = g[:, HID:]
        else:
            for m in range(8):
                f = m * 256
                gwd_ref[:, pl.ds(f, 256)] = dot_tn(
                    hs[:, 2 * HID :], xy[1, :, :, :, f : f + 256].reshape(STEPS * BLK, 256)
                ).astype(BF16)

    stage_gather(0)
    for i in range(STEPS + 5):
        if 0 <= i - 0 < STEPS:
            stage_forward(i - 0)
        if 0 <= i - 4 < STEPS:
            stage_pair(i - 4)
        if i + 1 < STEPS:
            stage_gather(i + 1)
        if 0 <= i - 2 < STEPS:
            stage_relay(i - 2)
        if 0 <= i - 3 < STEPS:
            stage_tokens(i - 3)
        if 0 <= i - 1 < STEPS:
            stage_hidden(i - 1)
        j = i - 5
        if 0 <= j < STEPS and (j % 2 == 0 or j == 7):
            stage_home((j + 1) // 2)
        if i == STEPS + 3:
            weight_grads(0)
            weight_grads(1)

    stage_join()
    weight_grads(2)
    total = acc[0, 0] + landed(0) + landed(1)
    gt_ref[...] = (total + landed(4) + landed(5)).astype(BF16)
    for cp in pending:
        cp.wait_send()


def store_kernel(a, b, c, d, oa, ob, oc, od, sems):
    copies = [
        pltpu.make_async_copy(src, dst, sems.at[i])
        for i, (src, dst) in enumerate(((a, oa), (b, ob), (c, oc), (d, od)))
    ]
    for cp in copies:
        cp.start()
    for cp in copies:
        cp.wait()


def store(arrays):
    anywhere = pl.BlockSpec(memory_space=pl.ANY)
    return pl.pallas_call(
        store_kernel,
        out_shape=tuple(jax.ShapeDtypeStruct(a.shape, a.dtype) for a in arrays),
        in_specs=[anywhere] * 4,
        out_specs=(anywhere,) * 4,
        scratch_shapes=[pltpu.SemaphoreType.DMA((4,))],
        compiler_params=pltpu.CompilerParams(vmem_limit_bytes=2**20),
        name="store_results",
    )(*arrays)


def local(tokens, cotangent, w_gate, w_up, w_down):
    dma = pltpu.SemaphoreType.DMA
    vm = pltpu.VMEM
    any_spec = pl.BlockSpec(memory_space=pl.ANY)
    vmem_spec = pl.BlockSpec(memory_space=pltpu.VMEM)
    results = pl.pallas_call(
        kernel,
        out_shape=(
            jax.ShapeDtypeStruct((TOK, FEAT), BF16),
            jax.ShapeDtypeStruct((FEAT, HID), BF16),
            jax.ShapeDtypeStruct((FEAT, HID), BF16),
            jax.ShapeDtypeStruct((HID, FEAT), BF16),
        ),
        in_specs=[vmem_spec, vmem_spec, any_spec, any_spec, any_spec],
        out_specs=(vmem_spec,) * 4,
        scratch_shapes=[
            vm((2, TOK, FEAT), BF16),
            vm((2, STEPS, 2, SUB, FEAT), BF16),
            vm((FEAT, 2 * HID), BF16),
            vm((HID, FEAT), BF16),
            vm((BLK, H3), F32),
            vm((STEPS, PIECE, H3), F32),
            vm((STEPS, BLK, H3), BF16),
            vm((STEPS, CN - 1, PIECE, H3), BF16),
            vm((STEPS, BLK, H3), BF16),
            vm((STEPS, 2, 2, TOK, FEAT), F32),
            vm((STEPS, 2, TOK, FEAT), F32),
            vm((5, 2, TOK, FEAT), BF16),
            vm((5, 2, TOK, FEAT), BF16),
            vm((6, TOK, FEAT), BF16),
            vm((6, TOK, FEAT), BF16),
            vm((2, TOK, HALF), BF16),
            vm((2, TOK, HALF), BF16),
            vm((5, 2, TOK, FEAT), F32),
            dma((3,)),
            dma(()),
            dma((3,)),
            dma((3,)),
            dma((7, 2)),
            dma((7, 2)),
            dma((STEPS,)),
            dma((STEPS,)),
            dma((STEPS, CN - 1)),
            dma((STEPS, CN - 1)),
            dma((STEPS, CN - 1)),
            dma((STEPS, CN - 1)),
            dma((STEPS, 2)),
            dma((STEPS, 2)),
            dma((5, 2)),
            dma((5, 2)),
            dma((6,)),
            dma((6,)),
            dma((2,)),
            dma((2,)),
        ],
        compiler_params=pltpu.CompilerParams(
            collective_id=0, has_side_effects=True, vmem_limit_bytes=48 * 2**20
        ),
        cost_estimate=pl.CostEstimate(
            flops=13 * 10**9, bytes_accessed=10**7, transcendentals=5 * 10**4
        ),
        name="swiglu_backward",
    )(tokens, cotangent, w_gate, w_up, w_down)
    return store(results)


def solution(mesh):
    placed = (P("row", "col"), P("row", "col"), P("col", "row"), P("col", "row"), P("row", "col"))
    return jax.shard_map(
        local,
        mesh=mesh,
        in_specs=placed,
        out_specs=(P("row", "col"), P("col", "row"), P("col", "row"), P("row", "col")),
        check_vma=False,
    )
```

```python
import jax
import jax.numpy as jnp
from jax import lax
from jax.experimental import pallas as pl
from jax.experimental.pallas import tpu as pltpu
from jax.sharding import PartitionSpec as P

MESH = pl.DeviceIdType.MESH
F32 = jnp.float32
BF16 = jnp.bfloat16

ZN = 8
CN = 8
STEPS = 8
SUB = 64
BLK = 2 * SUB
PIECE = BLK // CN
FEAT = 2048
HID = 384
H3 = 3 * HID
TOK = 32
HALF = FEAT // 2


def dot_nn(a, b):
    return lax.dot_general(a, b, (((1,), (0,)), ((), ())), preferred_element_type=F32)


def dot_nt(a, b):
    return lax.dot_general(a, b, (((1,), (1,)), ((), ())), preferred_element_type=F32)


def dot_tn(a, b):
    return lax.dot_general(a, b, (((0,), (0,)), ((), ())), preferred_element_type=F32)


def kernel(
    x_ref, dy_ref, wg_ref, wu_ref, wd_ref,
    gt_ref, gwg_ref, gwu_ref, gwd_ref,
    t_own, xy, wgu, wd, pf, own, pb, rb, hid, gf, r1, s2, r2, s3, rd, s4, r4, acc,
    w_sem, t_sem, ex_s, ex_r, ring_s, ring_r, sib_s, sib_r,
    b_s, b_r, c_s, c_r, d1_s, d1_r, d2_s, d2_r, d3_s, d3_r, d4_s, d4_r,
):
    row = lax.axis_index("row")
    col = lax.axis_index("col")
    yh, z, c = row // (2 * ZN), (row // 2) % ZN, row % 2

    def at(dz=0, dyh=0, dc=0):
        return (((yh + dyh) % 2) * (2 * ZN) + ((z + dz + ZN) % ZN) * 2 + (c + dc) % 2, col)

    def colpeer(r):
        return (row, (col + r) % CN)

    def colat(dx=0, dyl=0):
        return ((col // 2 + dx) % (CN // 2)) * 2 + (col % 2 + dyl) % 2

    def rows16(q):
        return pl.ds(pl.multiple_of(q * PIECE, PIECE), PIECE)

    sib, partner, cross = at(dc=1), at(dyh=1), at(dyh=1, dc=1)

    loads = [
        pltpu.make_async_copy(wg_ref, wgu.at[:, pl.ds(0, HID)], w_sem.at[0]),
        pltpu.make_async_copy(wu_ref, wgu.at[:, pl.ds(HID, HID)], w_sem.at[1]),
        pltpu.make_async_copy(wd_ref, wd, w_sem.at[2]),
    ]
    for cp in loads:
        cp.start()

    barrier = pltpu.get_barrier_semaphore()
    greet = [sib, partner, cross]
    greet += [at(dz=k) for k in (1, 2, -2, -1)]
    greet += [colpeer(r) for r in range(1, CN)]
    for d in greet:
        pl.semaphore_signal(barrier, inc=1, device_id=d, device_id_type=MESH)
    t_own[0] = x_ref[...]
    t_own[1] = dy_ref[...]
    pl.semaphore_wait(barrier, len(greet))

    def remote(src, dst, ss, rs, dev):
        return pltpu.make_async_remote_copy(
            src_ref=src, dst_ref=dst, send_sem=ss, recv_sem=rs, device_id=dev, device_id_type=MESH
        )

    pending = []

    def sent(keep):
        while len(pending) > keep:
            pending.pop(0).wait_send()

    def go(cp):
        cp.start()
        pending.append(cp)
        return cp

    mine = pl.ds(pl.multiple_of(c * TOK, TOK), TOK)
    go(remote(t_own.at[1 - c], xy.at[1 - c, 0, 0, mine], ex_s.at[0], ex_r.at[0], sib))
    go(remote(t_own.at[c], xy.at[c, 0, 1, mine], ex_s.at[1], ex_r.at[1], partner))
    go(remote(t_own.at[1 - c], xy.at[1 - c, 0, 1, mine], ex_s.at[2], ex_r.at[2], cross))
    keep = pltpu.make_async_copy(t_own.at[c], xy.at[c, 0, 0, mine], t_sem)
    keep.start()

    theirs = pl.ds(pl.multiple_of((1 - c) * TOK, TOK), TOK)

    def arrived(src, dst, ss, rs):
        remote(src, dst, ss, rs, sib).wait_recv()

    nxt = (at(dz=1), at(dz=-1))

    def send_ring(src_step, src_half, dst_step, d):
        go(
            remote(
                xy.at[c, src_step, src_half], xy.at[c, dst_step, d],
                ring_s.at[dst_step - 1, d], ring_r.at[dst_step - 1, d], nxt[d],
            )
        )

    def stage_gather(s):
        if s == 0:
            keep.wait()
            arrived(t_own.at[0], xy.at[c, 0, 0, theirs], ex_s.at[0], ex_r.at[0])
            send_ring(0, 0, 1, 0)
            send_ring(0, 0, 1, 1)
            arrived(t_own.at[0], xy.at[c, 0, 1, mine], ex_s.at[1], ex_r.at[1])
            arrived(t_own.at[0], xy.at[c, 0, 1, theirs], ex_s.at[2], ex_r.at[2])
            send_ring(0, 1, 2, 0)
            send_ring(0, 1, 2, 1)
        else:
            for d in range(2):
                arrived(xy.at[c, s, d], xy.at[c, s, d], ring_s.at[s - 1, d], ring_r.at[s - 1, d])
                if s <= 4 or (s == 5 and d == 0) or (s == 6 and d == 1):
                    send_ring(s, d, 7 if s >= 5 else s + 2, d)
        go(remote(xy.at[c, s], xy.at[c, s], sib_s.at[s], sib_r.at[s], sib))

    me16 = pl.ds(pl.multiple_of(col * PIECE, PIECE), PIECE)

    def stage_forward(s):
        arrived(xy.at[1 - c, s], xy.at[1 - c, s], sib_s.at[s], sib_r.at[s])
        if s == 0:
            for cp in loads:
                cp.wait()
        pf[:, : 2 * HID] = dot_nn(xy[0, s].reshape(BLK, FEAT), wgu[...])
        pf[:, 2 * HID :] = dot_nt(xy[1, s].reshape(BLK, FEAT), wd[...])
        pb[s] = pf[...].astype(BF16)
        own[s] = pf[me16, :]
        for r in range(1, CN):
            q = (col + r) % CN
            go(
                remote(
                    pb.at[s, pl.ds(pl.multiple_of(q * PIECE, PIECE), PIECE)], rb.at[s, r - 1],
                    b_s.at[s, r - 1], b_r.at[s, r - 1], colpeer(r),
                )
            )

    def stage_hidden(s):
        total = own[s]
        for r in range(1, CN):
            arrived(rb.at[s, r - 1], rb.at[s, r - 1], b_s.at[s, r - 1], b_r.at[s, r - 1])
            total = total + rb[s, r - 1].astype(F32)
        gate_value = total[:, :HID]
        up_value = total[:, HID : 2 * HID]
        grad_act = total[:, 2 * HID :]
        sig = jax.nn.sigmoid(gate_value)
        silu = gate_value * sig
        hid[s, me16, pl.ds(0, HID)] = (
            grad_act * up_value * sig * (1.0 + gate_value * (1.0 - sig))
        ).astype(BF16)
        hid[s, me16, pl.ds(HID, HID)] = (grad_act * silu).astype(BF16)
        hid[s, me16, pl.ds(2 * HID, HID)] = (silu * up_value).astype(BF16)
        go(remote(hid.at[s, me16], hid.at[s, me16], c_s.at[s, 0], c_r.at[s, 0], (row, colat(dyl=1))))
        send_x(s, me16, 0)

    def send_x(s, rows, base):
        for dx in range(1, CN // 2):
            q = base + dx
            go(remote(hid.at[s, rows], hid.at[s, rows], c_s.at[s, q], c_r.at[s, q], (row, colat(dx=dx))))

    def stage_relay(s):
        piece = rows16(colat(dyl=1))
        arrived(hid.at[s, piece], hid.at[s, piece], c_s.at[s, 0], c_r.at[s, 0])
        send_x(s, piece, 3)

    def stage_tokens(s):
        for dx in range(1, CN // 2):
            for dyl in range(2):
                piece = hid.at[s, rows16(colat(dx=CN // 2 - dx, dyl=dyl))]
                q = 3 * dyl + dx
                arrived(piece, piece, c_s.at[s, q], c_r.at[s, q])
        gf[s] = dot_nt(hid[s, :, : 2 * HID], wgu[...]).reshape(2, 2, TOK, FEAT)
        for d in range(2):
            go(remote(gf.at[s, d, 1 - c], r1.at[s, d], d1_s.at[s, d], d1_r.at[s, d], sib))

    def stage_pair(s):
        for d in range(2):
            arrived(r1.at[s, d], r1.at[s, d], d1_s.at[s, d], d1_r.at[s, d])
        for d in range(2):
            v = gf[s, d, c] + r1[s, d]
            other = d == 1 if s in (0, 7) else s % 2 == 0
            if other:
                k = (s + 1) // 2
                s2[k, d] = v.astype(BF16)
                go(remote(s2.at[k, d], r2.at[k, d], d2_s.at[k, d], d2_r.at[k, d], partner))
            else:
                acc[(s + 1) // 2, d] = v

    def hop(slot, dz):
        go(remote(s3.at[slot], rd.at[slot], d3_s.at[slot], d3_r.at[slot], at(dz=dz)))

    def landed(slot):
        arrived(rd.at[slot], rd.at[slot], d3_s.at[slot], d3_r.at[slot])
        return rd[slot].astype(F32)

    def stage_home(k):
        if k in (0, 4):
            arrived(r2.at[k, 1], r2.at[k, 1], d2_s.at[k, 1], d2_r.at[k, 1])
            v = acc[k, 0] + r2[k, 1].astype(F32)
            if k == 0:
                acc[0, 0] = v
                return
            for d in range(2):
                s4[d] = v[:, d * HALF : (d + 1) * HALF].astype(BF16)
                go(remote(s4.at[d], r4.at[d], d4_s.at[d], d4_r.at[d], at(dz=2 if d else -2)))
            return
        for d in range(2):
            arrived(r2.at[k, d], r2.at[k, d], d2_s.at[k, d], d2_r.at[k, d])
            v = acc[k, d] + r2[k, d].astype(F32)
            if k == 2:
                acc[2, d] = v
            else:
                slot = k - 1 + d
                s3[slot] = v.astype(BF16)
                hop(slot, 1 if d else -1)

    def stage_join():
        for d in range(2):
            acc[2, d] = acc[2, d] + landed(2 + d)
        for d in range(2):
            part = pl.ds(d * HALF, HALF)
            arrived(r4.at[d], r4.at[d], d4_s.at[d], d4_r.at[d])
            acc[2, d, :, part] = acc[2, d, :, part] + r4[d].astype(F32)
            s3[4 + d] = acc[2, d].astype(BF16)
            hop(4 + d, 2 if d else -2)

    def weight_grads(which):
        hs = hid[...].reshape(STEPS * BLK, H3)
        if which < 2:
            for m in range(4):
                f = (which * 4 + m) * 256
                g = dot_tn(
                    xy[0, :, :, :, f : f + 256].reshape(STEPS * BLK, 256), hs[:, : 2 * HID]
                ).astype(BF16)
                gwg_ref[pl.ds(f, 256), :] = g[:, :HID]
                gwu_ref[pl.ds(f, 256), :] = g[:, HID:]
        else:
            for m in range(8):
                f = m * 256
                gwd_ref[:, pl.ds(f, 256)] = dot_tn(
                    hs[:, 2 * HID :], xy[1, :, :, :, f : f + 256].reshape(STEPS * BLK, 256)
                ).astype(BF16)

    stage_gather(0)
    for i in range(STEPS + 5):
        if 0 <= i - 0 < STEPS:
            stage_forward(i - 0)
        if 0 <= i - 4 < STEPS:
            stage_pair(i - 4)
        if i + 1 < STEPS:
            stage_gather(i + 1)
        if 0 <= i - 2 < STEPS:
            stage_relay(i - 2)
        if 0 <= i - 3 < STEPS:
            stage_tokens(i - 3)
        if 0 <= i - 1 < STEPS:
            stage_hidden(i - 1)
        j = i - 5
        if 0 <= j < STEPS and (j % 2 == 0 or j == 7):
            stage_home((j + 1) // 2)
        if i == STEPS + 3:
            weight_grads(0)
            weight_grads(1)
            sent(12)

    stage_join()
    weight_grads(2)
    total = acc[0, 0] + landed(0) + landed(1)
    gt_ref[...] = (total + landed(4) + landed(5)).astype(BF16)
    sent(0)


def store_kernel(a, b, c, d, oa, ob, oc, od, sems):
    copies = [
        pltpu.make_async_copy(src, dst, sems.at[i])
        for i, (src, dst) in enumerate(((a, oa), (b, ob), (c, oc), (d, od)))
    ]
    for cp in copies:
        cp.start()
    for cp in copies:
        cp.wait()


def store(arrays):
    anywhere = pl.BlockSpec(memory_space=pl.ANY)
    return pl.pallas_call(
        store_kernel,
        out_shape=tuple(jax.ShapeDtypeStruct(a.shape, a.dtype) for a in arrays),
        in_specs=[anywhere] * 4,
        out_specs=(anywhere,) * 4,
        scratch_shapes=[pltpu.SemaphoreType.DMA((4,))],
        compiler_params=pltpu.CompilerParams(vmem_limit_bytes=2**20),
        name="store_results",
    )(*arrays)


def local(tokens, cotangent, w_gate, w_up, w_down):
    dma = pltpu.SemaphoreType.DMA
    vm = pltpu.VMEM
    any_spec = pl.BlockSpec(memory_space=pl.ANY)
    vmem_spec = pl.BlockSpec(memory_space=pltpu.VMEM)
    results = pl.pallas_call(
        kernel,
        out_shape=(
            jax.ShapeDtypeStruct((TOK, FEAT), BF16),
            jax.ShapeDtypeStruct((FEAT, HID), BF16),
            jax.ShapeDtypeStruct((FEAT, HID), BF16),
            jax.ShapeDtypeStruct((HID, FEAT), BF16),
        ),
        in_specs=[vmem_spec, vmem_spec, any_spec, any_spec, any_spec],
        out_specs=(vmem_spec,) * 4,
        scratch_shapes=[
            vm((2, TOK, FEAT), BF16),
            vm((2, STEPS, 2, SUB, FEAT), BF16),
            vm((FEAT, 2 * HID), BF16),
            vm((HID, FEAT), BF16),
            vm((BLK, H3), F32),
            vm((STEPS, PIECE, H3), F32),
            vm((STEPS, BLK, H3), BF16),
            vm((STEPS, CN - 1, PIECE, H3), BF16),
            vm((STEPS, BLK, H3), BF16),
            vm((STEPS, 2, 2, TOK, FEAT), F32),
            vm((STEPS, 2, TOK, FEAT), F32),
            vm((5, 2, TOK, FEAT), BF16),
            vm((5, 2, TOK, FEAT), BF16),
            vm((6, TOK, FEAT), BF16),
            vm((6, TOK, FEAT), BF16),
            vm((2, TOK, HALF), BF16),
            vm((2, TOK, HALF), BF16),
            vm((5, 2, TOK, FEAT), F32),
            dma((3,)),
            dma(()),
            dma((3,)),
            dma((3,)),
            dma((7, 2)),
            dma((7, 2)),
            dma((STEPS,)),
            dma((STEPS,)),
            dma((STEPS, CN - 1)),
            dma((STEPS, CN - 1)),
            dma((STEPS, CN - 1)),
            dma((STEPS, CN - 1)),
            dma((STEPS, 2)),
            dma((STEPS, 2)),
            dma((5, 2)),
            dma((5, 2)),
            dma((6,)),
            dma((6,)),
            dma((2,)),
            dma((2,)),
        ],
        compiler_params=pltpu.CompilerParams(
            collective_id=0, has_side_effects=True, vmem_limit_bytes=48 * 2**20
        ),
        cost_estimate=pl.CostEstimate(
            flops=13 * 10**9, bytes_accessed=10**7, transcendentals=5 * 10**4
        ),
        name="swiglu_backward",
    )(tokens, cotangent, w_gate, w_up, w_down)
    return store(results)


def solution(mesh):
    placed = (P("row", "col"), P("row", "col"), P("col", "row"), P("col", "row"), P("row", "col"))
    return jax.shard_map(
        local,
        mesh=mesh,
        in_specs=placed,
        out_specs=(P("row", "col"), P("col", "row"), P("col", "row"), P("row", "col")),
        check_vma=False,
    )
```
